128 devices in a mesh: wide: 16 (over y, z), narrow: 8 (over x, core).
Axes of the slice: x: 4, y: 4, z: 4, core: 2. Of those that a mesh axis runs over, the one named last changes fastest.
Arguments:
- hidden: bfloat16 [128, 16384], P('narrow', 'wide'), may hold values from -6 to 6
- gain: bfloat16 [16384], P('wide'), may hold values from 0.5 to 1.5
- sign_in: int32 [16384], P('wide'), may hold values from 0 to 1
- qkv_weight: bfloat16 [16384, 18432], P('wide', 'narrow'), may hold values from -0.046875 to 0.046875
- out_weight: bfloat16 [16384, 16384], P('narrow', 'wide'), may hold values from -0.046875 to 0.046875
- sign_attn: int32 [16384], P('narrow'), may hold values from 0 to 1
- key_cache: bfloat16 [128, 8, 4096, 128], P('wide', 'narrow'), may hold values from -512 to 512, as said below
- value_cache: bfloat16 [128, 8, 4096, 128], P('wide', 'narrow'), may hold values from -6 to 6
- lengths: int32 [128], P('wide'), may hold values from 1024 to 4096
Outputs:
- layer_out: bfloat16 [128, 16384], P('narrow', 'wide')
The draws below stay inside these ranges and needn't reach their ends.
Inputs may be any that keep to these rules, and one draw needn't show every extreme that they name: `key_cache`: cached keys mostly of magnitude about 2, with some slots far larger in the hidden draw.
All inputs are finite; a program needn't handle non-finite values. Where the reference program divides by a largest or mean magnitude, that divisor is 1e-20 or more.
Results may differ from the reference program's by a relative error of at most 0.018.
Values may be sent and summed in bfloat16 or wider, within the bound.
No kernel may reach another device: no remote copies, remote signals or barrier semaphores. Data moves between devices by JAX's collectives and lax.ppermute only.
A program may use at most 128 MiB of HBM per device.

```python
import math
import jax
import jax.numpy as jnp
from jax import lax

D = 16384
HQ = 128
KVH = 8
HD = 128
S = 4096
LISTS = 128
QG = 16


def draw_key_cache(key, part):
    normal_keys = jax.random.normal(jax.random.fold_in(key, 11), (LISTS, KVH, S, HD), jnp.float32) * 2.0
    normal_keys = jnp.clip(normal_keys, -12.0, 12.0)
    return normal_keys.astype(jnp.bfloat16)


def touch_ends(result, own_key, least, largest):
    extent = result.shape
    index_at = [jax.random.randint(jax.random.fold_in(own_key, axis), (), 0, extent[axis]) for axis in range(len(extent))]
    result = result.at[tuple(index_at)].set(least)
    longest = extent.index(max(extent))
    index_at[longest] = (index_at[longest] + 1) % extent[longest]
    return result.at[tuple(index_at)].set(largest)


def shard_levels(rng, extent, cuts, smallest, top_value):
    level, own = 1.0, jax.random.fold_in(rng, 6)
    for position, shards_of in cuts:
        heights = jnp.exp(jax.random.uniform(jax.random.fold_in(own, position), (shards_of,), jnp.float32, smallest / len(cuts), top_value / len(cuts)))
        level = level * jnp.repeat(heights, extent[position] // shards_of).reshape([-1 if axis == position else 1 for axis in range(len(extent))])
    return level


def bell_draw(rng, shape, deviation, reach, cuts=(), kind=jnp.bfloat16):
    level = shard_levels(rng, shape, cuts, -0.22, 0.18) if cuts else 1.0
    entries = jax.random.normal(rng, shape, jnp.float32) * deviation * level
    return jnp.minimum(jnp.maximum(entries, -reach), reach).astype(kind)


def setup_inputs(seed: int = 0) -> dict:
    key_list = jax.random.split(jax.random.key(seed), 10)
    hidden = bell_draw(key_list[0], (LISTS, D), 1.0, 6.0, ((0, 8), (1, 16)))
    gain = jnp.clip(1.0 + 0.1 * jax.random.normal(key_list[1], (D,), jnp.float32), 0.5, 1.5).astype(jnp.bfloat16)
    sign_in = touch_ends(jax.random.randint(key_list[2], (D,), 0, 2), jax.random.fold_in(key_list[2], 1), 0, 1).astype(jnp.int32)
    qkv_weight = bell_draw(key_list[3], (D, KVH * (QG + 2) * HD), D ** -0.5, 0.046875, ((0, 16), (1, 8)))
    out_weight = bell_draw(key_list[4], (HQ * HD, D), (HQ * HD) ** -0.5, 0.046875, ((0, 8), (1, 16)))
    sign_attn = touch_ends(jax.random.randint(key_list[5], (HQ * HD,), 0, 2), jax.random.fold_in(key_list[5], 1), 0, 1).astype(jnp.int32)
    key_cache = draw_key_cache(jax.random.fold_in(key_list[9], 71), 0)
    value_cache = bell_draw(key_list[7], (LISTS, KVH, S, HD), 1.0, 6.0, ((0, 16), (1, 8)))
    lengths = touch_ends(jax.random.randint(key_list[8], (LISTS,), S // 4, S + 1), jax.random.fold_in(key_list[8], 1), S // 4, S).astype(jnp.int32)
    return {"hidden": hidden, "gain": gain, "sign_in": sign_in, "qkv_weight": qkv_weight, "out_weight": out_weight, "sign_attn": sign_attn, "key_cache": key_cache, "value_cache": value_cache, "lengths": lengths}


ROPE_BASE = 500000.0

def hadamard(order):
    places = jnp.arange(order, dtype=jnp.int32)
    common = places[:, None] & places[None, :]
    parity = jnp.zeros((order, order), jnp.int32)
    for bit_pos in range(order.bit_length() - 1):
        parity = parity ^ common >> bit_pos & 1
    return (1 - 2 * parity).astype(jnp.float32) / math.sqrt(order)

def rotate_blocks(values, sign_bits, width):
    signs = (2 * sign_bits - 1).astype(jnp.float32)
    blocks = (values * signs).reshape(values.shape[:-1] + (values.shape[-1] // width, width))
    turned = jnp.einsum('...bk,kj->...bj', blocks, hadamard(width), precision=lax.Precision.HIGHEST)
    scales = (lax.optimization_barrier(jnp.max(jnp.abs(turned), axis=-1)) + 1e-06).astype(jnp.bfloat16)
    payload = (turned / scales.astype(jnp.float32)[..., None]).astype(jnp.bfloat16)
    return (payload, scales)

def rotary(vectors, positions):
    half_width = vectors.shape[-1] // 2
    frequency = jnp.exp(jnp.arange(half_width, dtype=jnp.float32) * (-2.0 * math.log(ROPE_BASE) / vectors.shape[-1]))
    angles = positions.astype(jnp.float32)[:, None] * frequency[None, :]
    cosine = jnp.cos(angles)[:, None, :]
    sines = jnp.sin(angles)[:, None, :]
    lower_half = vectors[..., :half_width]
    upper_half = vectors[..., half_width:]
    return jnp.concatenate([lower_half * cosine - upper_half * sines, upper_half * cosine + lower_half * sines], axis=-1)

def reference(hidden, gain, sign_in, qkv_weight, out_weight, sign_attn, key_cache, value_cache, lengths):
    rows = hidden.astype(jnp.float32)
    factor = lax.rsqrt(lax.optimization_barrier(jnp.sum(rows * rows, axis=1)) / D + 1e-05)
    normed = rows * factor[:, None] * gain.astype(jnp.float32)[None, :]
    payload, scales = rotate_blocks(normed, sign_in, HD)
    weight_blocks = qkv_weight.reshape(D // HD, HD, qkv_weight.shape[1])

    def add_block(total, inputs):
        block_rows, block_scale, block_weight = inputs
        product = jnp.dot(block_rows, block_weight, preferred_element_type=jnp.float32)
        return (total + block_scale.astype(jnp.float32)[:, None] * product, None)
    start_total = jnp.zeros((LISTS, qkv_weight.shape[1]), jnp.float32)
    projected, _ = lax.scan(add_block, start_total, (jnp.swapaxes(payload, 0, 1), jnp.swapaxes(scales, 0, 1), weight_blocks))
    grouped = projected.reshape(LISTS, KVH, QG + 2, HD)
    queries = rotary(grouped[:, :, :QG, :].reshape(LISTS, KVH * QG, HD), lengths)
    queries = queries.astype(jnp.bfloat16).reshape(LISTS, KVH, QG, HD)
    keys_new = rotary(grouped[:, :, QG, :], lengths).astype(jnp.bfloat16)
    values_new = grouped[:, :, QG + 1, :].astype(jnp.bfloat16)
    inverse_root = 1.0 / math.sqrt(HD)

    def attend(inputs):
        query, key_new, value_new, keys, values, length = inputs
        query_f = query.astype(jnp.float32)
        scores = jnp.einsum('gqk,gsk->gqs', query_f, keys.astype(jnp.float32)) * inverse_root
        fresh = jnp.einsum('gqk,gk->gq', query_f, key_new.astype(jnp.float32)) * inverse_root
        live = jnp.arange(S, dtype=jnp.int32) < length
        scores = jnp.where(live[None, None, :], scores, -1e+30)
        peak = jnp.maximum(lax.optimization_barrier(jnp.max(scores, axis=-1)), fresh)
        weights = jnp.where(live[None, None, :], jnp.exp(scores - peak[..., None]), 0.0)
        weight_new = jnp.exp(fresh - peak)
        denom_sum = lax.optimization_barrier(jnp.sum(weights, axis=-1)) + weight_new
        probs = (weights / denom_sum[..., None]).astype(jnp.bfloat16)
        prob_new = (weight_new / denom_sum).astype(jnp.bfloat16)
        mixed = jnp.einsum('gqs,gsk->gqk', probs.astype(jnp.float32), values.astype(jnp.float32))
        return mixed + prob_new.astype(jnp.float32)[..., None] * value_new.astype(jnp.float32)[:, None, :]
    attended = lax.map(attend, (queries, keys_new, values_new, key_cache, value_cache, lengths))
    out_blocks, out_scale = rotate_blocks(attended.reshape(LISTS, HQ * HD), sign_attn, HD)
    head_weights = out_weight.reshape(HQ, HD, D)

    def add_head(total, inputs):
        head_rows, head_scale, head_weight = inputs
        product = jnp.dot(head_rows, head_weight, preferred_element_type=jnp.float32)
        return (total + head_scale.astype(jnp.float32)[:, None] * product, None)
    mixed, _ = lax.scan(add_head, jnp.zeros((LISTS, D), jnp.float32), (jnp.swapaxes(out_blocks, 0, 1), jnp.swapaxes(out_scale, 0, 1), head_weights))
    return (rows + mixed).astype(jnp.bfloat16)
```

```python
import math

import jax
import jax.numpy as jnp
from jax import lax
from jax.experimental import pallas as pl
from jax.experimental.pallas import tpu as pltpu
from jax.sharding import Mesh
from jax.sharding import PartitionSpec as P

D = 16384
HD = 128
QG = 16
WIDE = ("y", "z")
ROPE_BASE = 500000.0
EXTRA = 128
MIB = 1 << 20
VMEM = pl.BlockSpec(memory_space=pltpu.VMEM)
SMEM = pl.BlockSpec(memory_space=pltpu.SMEM)
HBM = pl.BlockSpec(memory_space=pl.ANY)
F32 = jnp.float32
BF16 = jnp.bfloat16


def hadamard_signs():
    common = lax.broadcasted_iota(jnp.int32, (HD, HD), 0) & lax.broadcasted_iota(jnp.int32, (HD, HD), 1)
    common = common ^ (common >> 4)
    common = common ^ (common >> 2)
    common = common ^ (common >> 1)
    return (1 - 2 * (common & 1)).astype(F32).astype(BF16)


def two_piece_dot(values, matrix):
    high = values.astype(BF16)
    low = (values - high.astype(F32)).astype(BF16)
    return jnp.dot(high, matrix, preferred_element_type=F32) + jnp.dot(low, matrix, preferred_element_type=F32)


def rotate_in_kernel(own_ref, other_ref, gain_ref, sign_ref, out_ref):
    features = own_ref.shape[1]
    matrix = hadamard_signs()
    steer = gain_ref[...].astype(F32) * (2 * sign_ref[...] - 1).astype(F32)
    lane = lax.broadcasted_iota(jnp.int32, (16, EXTRA), 1)
    for at, ref in enumerate((own_ref, other_ref)):
        rows = ref[...].astype(F32)
        squares = jnp.sum(rows * rows, axis=1, keepdims=True)
        first = squares.astype(BF16).astype(F32)
        second = (squares - first).astype(BF16).astype(F32)
        third = squares - first - second
        pieces = jnp.where(lane == 0, first, jnp.where(lane == 1, second, jnp.where(lane == 2, third, 0.0)))
        out_ref[16 * at : 16 * at + 16, features:] = pieces.astype(BF16)
        steered = rows * steer
        for b in range(features // HD):
            turned = two_piece_dot(steered[:, b * HD : (b + 1) * HD], matrix) * (1.0 / math.sqrt(HD))
            out_ref[16 * at : 16 * at + 16, b * HD : (b + 1) * HD] = turned.astype(BF16)


def project_kernel(place_ref, x0, x1, x2, x3, weight_hbm, out_ref, weight, sems):
    parts, width = 3, weight.shape[1] // 3
    features = weight.shape[0]

    def fetch(i):
        cols = pl.ds(i * width, width)
        return pltpu.make_async_copy(weight_hbm.at[:, cols], weight.at[:, cols], sems.at[i])

    for i in range(parts):
        fetch(i).start()
    x, c = place_ref[0], place_ref[1]
    received = (x0, x1, x2, x3)
    targets = []
    for s in range(4):
        for other in range(2):
            core = c if other == 0 else 1 - c
            source = 2 * ((x - s) & 3) + core
            targets += [2 * source, 2 * source + 1]
    for s in range(4):
        extra = received[s][:, features:].astype(F32)
        for j in range(4):
            out_ref[targets[4 * s + j], :, weight.shape[1] :] = extra[8 * j : 8 * j + 8].astype(BF16)
    rows = jnp.concatenate([r[:, :features] for r in received], axis=0)
    for i in range(parts):
        fetch(i).wait()
        product = jnp.dot(rows, weight[:, i * width : (i + 1) * width], preferred_element_type=F32)
        for j in range(16):
            out_ref[targets[j], :, i * width : (i + 1) * width] = product[8 * j : 8 * j + 8].astype(BF16)


CHUNK = 1024


def attend_kernel(
    lengths_ref, arrived_ref, cos_ref, sin_ref, sign_ref, key_hbm, value_hbm, out_ref,
    keys, values, queries, scores, attended, sems,
):
    lists = lengths_ref.shape[0]
    slots = keys.shape[1]
    chunks = slots // CHUNK

    def fetch(which, pair, half, chunk):
        source, target = ((key_hbm, keys), (value_hbm, values))[which]
        span = pl.ds(chunk * CHUNK, CHUNK)
        return pltpu.make_async_copy(
            source.at[2 * pair + half, 0, span, :],
            target.at[pair, span, pl.ds(half * HD, HD)],
            sems.at[which, pair, half, chunk],
        )

    longest = [jnp.maximum(lengths_ref[2 * p], lengths_ref[2 * p + 1]) for p in range(lists // 2)]
    for pair in range(lists // 2):
        for chunk in range(chunks):

            @pl.when(chunk * CHUNK < longest[pair])
            def _():
                for which in range(2):
                    for half in range(2):
                        fetch(which, pair, half, chunk).start()

    total = arrived_ref[0].astype(F32)
    for w in range(1, arrived_ref.shape[0]):
        total = total + arrived_ref[w].astype(F32)
    columns = (QG + 2) * HD
    squares = jnp.sum(total[:, columns:], axis=1, keepdims=True)
    factor = lax.rsqrt(squares * (1.0 / D) + 1e-05)
    cosine, sine = cos_ref[...], sin_ref[...]
    for h in range(QG + 2):
        vector = total[:, h * HD : (h + 1) * HD] * factor
        if h <= QG:
            vector = vector * cosine + pltpu.roll(vector, HD // 2, 1) * sine
        queries[:, h, :] = vector.astype(BF16).astype(F32)

    scale = 1.0 / math.sqrt(HD)
    row = lax.broadcasted_iota(jnp.int32, (2 * QG, 1), 0)
    for pair in range(lists // 2):
        first, second = queries[2 * pair], queries[2 * pair + 1]
        q_both = jnp.concatenate([first[:QG], second[:QG]], axis=0)
        blank = jnp.zeros((QG, HD), F32)
        q_wide = jnp.concatenate(
            [jnp.concatenate([first[:QG], blank], axis=1), jnp.concatenate([blank, second[:QG]], axis=1)], axis=0
        ).astype(BF16)
        k_new = jnp.concatenate(
            [jnp.broadcast_to(v[QG : QG + 1], (QG, HD)) for v in (first, second)], axis=0
        )
        v_new = jnp.concatenate(
            [jnp.broadcast_to(v[QG + 1 : QG + 2], (QG, HD)) for v in (first, second)], axis=0
        )
        fresh = jnp.sum(q_both * k_new, axis=1, keepdims=True) * scale
        length = jnp.where(row < QG, lengths_ref[2 * pair], lengths_ref[2 * pair + 1])
        live_chunks = (longest[pair] + CHUNK - 1) // CHUNK

        def score(chunk, peak):
            for half in range(2):
                fetch(0, pair, half, chunk).wait()
            start = pl.multiple_of(chunk * CHUNK, CHUNK)
            block = lax.dot_general(
                q_wide, keys[pair, pl.ds(start, CHUNK), :], (((1,), (1,)), ((), ())), preferred_element_type=F32
            )
            slot = lax.broadcasted_iota(jnp.int32, (2 * QG, CHUNK), 1) + start
            block = jnp.where(slot < length, block * scale, -1e30)
            scores[:, pl.ds(start, CHUNK)] = block
            for t in range(CHUNK // HD):
                peak = jnp.maximum(peak, block[:, t * HD : (t + 1) * HD])
            return peak

        peak = lax.fori_loop(0, live_chunks, score, jnp.full((2 * QG, HD), -1e30, F32))
        peak = jnp.maximum(jnp.max(peak, axis=1, keepdims=True), fresh)

        def mix(chunk, carry):
            mass, mixed = carry
            for half in range(2):
                fetch(1, pair, half, chunk).wait()
            start = pl.multiple_of(chunk * CHUNK, CHUNK)
            weight = jnp.exp(scores[:, pl.ds(start, CHUNK)] - peak)
            for t in range(CHUNK // HD):
                mass = mass + weight[:, t * HD : (t + 1) * HD]
            mixed = mixed + jnp.dot(
                weight.astype(BF16), values[pair, pl.ds(start, CHUNK), :], preferred_element_type=F32
            )
            return mass, mixed

        mass, mixed = lax.fori_loop(
            0, live_chunks, mix, (jnp.zeros((2 * QG, HD), F32), jnp.zeros((2 * QG, 2 * HD), F32))
        )
        weight_new = jnp.exp(fresh - peak)
        denominator = jnp.sum(mass, axis=1, keepdims=True) + weight_new
        own = jnp.concatenate([mixed[:QG, :HD], mixed[QG:, HD:]], axis=0)
        own = (own + weight_new.astype(BF16).astype(F32) * v_new) / denominator
        attended[2 * QG * pair : 2 * QG * (pair + 1), :] = own

    matrix = hadamard_signs()
    steered = []
    for h in range(QG):
        sign = (2 * sign_ref[:, h * HD : (h + 1) * HD] - 1).astype(F32)
        steered.append(attended[pl.ds(h, lists, stride=QG), :] * sign)
    turned = two_piece_dot(jnp.concatenate(steered, axis=0), matrix) * (1.0 / math.sqrt(HD))
    for h in range(QG):
        piece = turned[lists * h : lists * (h + 1)].astype(BF16)
        for w in range(out_ref.shape[0]):
            out_ref[w, :, h * HD : (h + 1) * HD] = piece


def mix_kernel(place_ref, rows_ref, weight_hbm, keep_ref, send_ref, weight, sems):
    parts, width = 4, weight.shape[1] // 4

    def fetch(i):
        cols = pl.ds(i * width, width)
        return pltpu.make_async_copy(weight_hbm.at[:, cols], weight.at[:, cols], sems.at[i])

    for i in range(parts):
        fetch(i).start()
    c = place_ref[1]
    rows = jnp.concatenate([rows_ref[x, c] for x in range(4)] + [rows_ref[x, 1 - c] for x in range(4)], axis=0)
    for i in range(parts):
        fetch(i).wait()
        product = jnp.dot(rows, weight[:, i * width : (i + 1) * width], preferred_element_type=F32)
        for x in range(4):
            keep_ref[x, :, i * width : (i + 1) * width] = product[16 * x : 16 * x + 16]
            send_ref[x, :, i * width : (i + 1) * width] = product[64 + 16 * x : 80 + 16 * x].astype(BF16)


def pair_sum_kernel(place_ref, keep_ref, got_ref, own_ref, s1, s2, s3):
    x = place_ref[0]
    own_ref[...] = keep_ref[x] + got_ref[x].astype(F32)
    for s, ref in ((1, s1), (2, s2), (3, s3)):
        to = (x + s) & 3
        ref[...] = (keep_ref[to] + got_ref[to].astype(F32)).astype(BF16)


def last_kernel(hidden_ref, own_ref, r1, r2, r3, out_ref):
    mixed = own_ref[...] + r1[...].astype(F32) + r2[...].astype(F32) + r3[...].astype(F32)
    out_ref[...] = (hidden_ref[...].astype(F32) + mixed).astype(BF16)


def params(limit):
    return pltpu.CompilerParams(vmem_limit_bytes=limit * MIB)


def along_x(value):
    return [lax.ppermute(value, "x", [(i, (i + s) % 4) for i in range(4)]) for s in (1, 2, 3)]


def across_cores(value):
    return lax.ppermute(value, "core", [(0, 1), (1, 0)])


def body(hidden, gain, sign_in, qkv_weight, out_weight, sign_attn, key_cache, value_cache, lengths):
    rows, features = hidden.shape
    columns = qkv_weight.shape[1]
    own_lists, _, slots, _ = key_cache.shape
    peers = lax.axis_size(WIDE)
    place = jnp.stack([lax.axis_index("x"), lax.axis_index("core")]).astype(jnp.int32)

    rotated = pl.pallas_call(
        rotate_in_kernel,
        out_shape=jax.ShapeDtypeStruct((2 * rows, features + EXTRA), BF16),
        in_specs=[VMEM] * 4,
        out_specs=VMEM,
        name="rotate_in",
    )(hidden, across_cores(hidden), gain.reshape(1, -1), sign_in.reshape(1, -1))
    partial = pl.pallas_call(
        project_kernel,
        out_shape=jax.ShapeDtypeStruct((peers, own_lists, columns + EXTRA), BF16),
        in_specs=[SMEM] + [VMEM] * 4 + [HBM],
        out_specs=VMEM,
        scratch_shapes=[pltpu.VMEM((features, columns), BF16), pltpu.SemaphoreType.DMA((3,))],
        compiler_params=params(16),
        name="project",
    )(place, rotated, *along_x(rotated), qkv_weight)
    arrived = lax.all_to_all(partial, WIDE, split_axis=0, concat_axis=0, tiled=True)

    frequency = jnp.exp(jnp.arange(HD // 2, dtype=F32) * (-2.0 * math.log(ROPE_BASE) / HD))
    angles = lengths.astype(F32)[:, None] * frequency[None, :]
    cosine, sine = jnp.cos(angles), jnp.sin(angles)
    sent = pl.pallas_call(
        attend_kernel,
        out_shape=jax.ShapeDtypeStruct((peers, own_lists, QG * HD), BF16),
        in_specs=[SMEM] + [VMEM] * 4 + [HBM] * 2,
        out_specs=VMEM,
        scratch_shapes=[
            pltpu.VMEM((own_lists // 2, slots, 2 * HD), BF16),
            pltpu.VMEM((own_lists // 2, slots, 2 * HD), BF16),
            pltpu.VMEM((own_lists, 24, HD), F32),
            pltpu.VMEM((2 * QG, slots), F32),
            pltpu.VMEM((own_lists * QG, HD), F32),
            pltpu.SemaphoreType.DMA((2, own_lists // 2, 2, slots // CHUNK)),
        ],
        compiler_params=params(32),
        name="attend",
    )(
        lengths,
        arrived,
        jnp.concatenate([cosine, cosine], axis=1),
        jnp.concatenate([-sine, sine], axis=1),
        sign_attn.reshape(1, -1),
        key_cache,
        value_cache,
    )
    gathered = lax.all_to_all(sent, WIDE, split_axis=0, concat_axis=0, tiled=True)
    keep, send = pl.pallas_call(
        mix_kernel,
        out_shape=(
            jax.ShapeDtypeStruct((4, rows, features), F32),
            jax.ShapeDtypeStruct((4, rows, features), BF16),
        ),
        in_specs=[SMEM, VMEM, HBM],
        out_specs=(VMEM, VMEM),
        scratch_shapes=[pltpu.VMEM(out_weight.shape, BF16), pltpu.SemaphoreType.DMA((4,))],
        compiler_params=params(16),
        name="mix",
    )(place, gathered.reshape(4, 2, rows, QG * HD), out_weight)
    own, *sends = pl.pallas_call(
        pair_sum_kernel,
        out_shape=(jax.ShapeDtypeStruct((rows, features), F32),)
        + (jax.ShapeDtypeStruct((rows, features), BF16),) * 3,
        in_specs=[SMEM, VMEM, VMEM],
        out_specs=(VMEM,) * 4,
        name="pair_sum",
    )(place, keep, across_cores(send))
    got = [
        lax.ppermute(v, "x", [(i, (i + s) % 4) for i in range(4)]) for s, v in zip((1, 2, 3), sends)
    ]
    return pl.pallas_call(
        last_kernel,
        out_shape=jax.ShapeDtypeStruct((rows, features), BF16),
        in_specs=[VMEM] * 5,
        out_specs=VMEM,
        name="last",
    )(hidden, own, *got)


def solution(mesh):
    split = Mesh(mesh.devices.reshape(4, 4, 4, 2), ("y", "z", "x", "core"))
    narrow = ("x", "core")
    placed = (
        P(narrow, WIDE),
        P(WIDE),
        P(WIDE),
        P(WIDE, narrow),
        P(narrow, WIDE),
        P(narrow),
        P(WIDE, narrow, None, None),
        P(WIDE, narrow, None, None),
        P(WIDE),
    )
    return jax.shard_map(
        body, mesh=split, in_specs=placed, out_specs=P(narrow, WIDE), check_vma=False
    )
```

```python
import math

import jax
import jax.numpy as jnp
from jax import lax
from jax.experimental import pallas as pl
from jax.experimental.pallas import tpu as pltpu
from jax.sharding import Mesh
from jax.sharding import PartitionSpec as P

D = 16384
HD = 128
QG = 16
WIDE = ("y", "z")
ROPE_BASE = 500000.0
EXTRA = 128
MIB = 1 << 20
VMEM = pl.BlockSpec(memory_space=pltpu.VMEM)
SMEM = pl.BlockSpec(memory_space=pltpu.SMEM)
HBM = pl.BlockSpec(memory_space=pl.ANY)
F32 = jnp.float32
BF16 = jnp.bfloat16


def hadamard_signs():
    common = lax.broadcasted_iota(jnp.int32, (HD, HD), 0) & lax.broadcasted_iota(jnp.int32, (HD, HD), 1)
    common = common ^ (common >> 4)
    common = common ^ (common >> 2)
    common = common ^ (common >> 1)
    return (1 - 2 * (common & 1)).astype(F32).astype(BF16)


def two_piece_dot(values, matrix):
    high = values.astype(BF16)
    low = (values - high.astype(F32)).astype(BF16)
    return jnp.dot(high, matrix, preferred_element_type=F32) + jnp.dot(low, matrix, preferred_element_type=F32)


def rotate_in_kernel(own_ref, other_ref, steer_ref, out_ref):
    features = own_ref.shape[1]
    matrix = hadamard_signs()
    steer = steer_ref[...]
    lane = lax.broadcasted_iota(jnp.int32, (16, EXTRA), 1)
    for at, ref in enumerate((own_ref, other_ref)):
        rows = ref[...].astype(F32)
        squares = jnp.sum(rows * rows, axis=1, keepdims=True)
        first = squares.astype(BF16).astype(F32)
        second = (squares - first).astype(BF16).astype(F32)
        third = squares - first - second
        pieces = jnp.where(lane == 0, first, jnp.where(lane == 1, second, jnp.where(lane == 2, third, 0.0)))
        out_ref[16 * at : 16 * at + 16, features:] = pieces.astype(BF16)
        steered = rows * steer
        for b in range(features // HD):
            turned = two_piece_dot(steered[:, b * HD : (b + 1) * HD], matrix) * (1.0 / math.sqrt(HD))
            out_ref[16 * at : 16 * at + 16, b * HD : (b + 1) * HD] = turned.astype(BF16)


def project_kernel(place_ref, x0, x1, x2, x3, weight, out_ref):
    parts, width = 3, weight.shape[1] // 3
    features = weight.shape[0]
    x, c = place_ref[0], place_ref[1]
    received = (x0, x1, x2, x3)
    targets = []
    for s in range(4):
        for other in range(2):
            core = c if other == 0 else 1 - c
            source = 2 * ((x - s) & 3) + core
            targets += [2 * source, 2 * source + 1]
    for s in range(4):
        extra = received[s][:, features:].astype(F32)
        for j in range(4):
            out_ref[targets[4 * s + j], :, weight.shape[1] :] = extra[8 * j : 8 * j + 8].astype(BF16)
    rows = jnp.concatenate([r[:, :features] for r in received], axis=0)
    for i in range(parts):
        product = jnp.dot(rows, weight[:, i * width : (i + 1) * width], preferred_element_type=F32)
        for j in range(16):
            out_ref[targets[j], :, i * width : (i + 1) * width] = product[8 * j : 8 * j + 8].astype(BF16)


CHUNK = 1024
COVER = (10, 10, 10)


def attend_kernel(
    lengths_ref, arrived_ref, cos_ref, sin_ref, sign_ref, keys, values, out_ref, queries, scores, attended
):
    lists = lengths_ref.shape[0]
    longest = [jnp.maximum(lengths_ref[2 * p], lengths_ref[2 * p + 1]) for p in range(lists // 2)]

    def wide(ref, pair, start):
        span = pl.ds(start, CHUNK)
        return jnp.concatenate([ref[2 * pair, 0, span, :], ref[2 * pair + 1, 0, span, :]], axis=1)

    total = arrived_ref[0].astype(F32)
    for w in range(1, arrived_ref.shape[0]):
        total = total + arrived_ref[w].astype(F32)
    columns = (QG + 2) * HD
    squares = jnp.sum(total[:, columns:], axis=1, keepdims=True)
    factor = lax.rsqrt(squares * (1.0 / D) + 1e-05)
    cosine, sine = cos_ref[...], sin_ref[...]
    for h in range(QG + 2):
        vector = total[:, h * HD : (h + 1) * HD] * factor
        if h <= QG:
            vector = vector * cosine + pltpu.roll(vector, HD // 2, 1) * sine
        queries[:, h, :] = vector.astype(BF16).astype(F32)

    scale = 1.0 / math.sqrt(HD)
    row = lax.broadcasted_iota(jnp.int32, (2 * QG, 1), 0)
    for pair in range(lists // 2):
        first, second = queries[2 * pair], queries[2 * pair + 1]
        q_both = jnp.concatenate([first[:QG], second[:QG]], axis=0)
        blank = jnp.zeros((QG, HD), F32)
        q_wide = jnp.concatenate(
            [jnp.concatenate([first[:QG], blank], axis=1), jnp.concatenate([blank, second[:QG]], axis=1)], axis=0
        ).astype(BF16)
        k_new = jnp.concatenate(
            [jnp.broadcast_to(v[QG : QG + 1], (QG, HD)) for v in (first, second)], axis=0
        )
        v_new = jnp.concatenate(
            [jnp.broadcast_to(v[QG + 1 : QG + 2], (QG, HD)) for v in (first, second)], axis=0
        )
        fresh = jnp.sum(q_both * k_new, axis=1, keepdims=True) * scale
        length = jnp.where(row < QG, lengths_ref[2 * pair], lengths_ref[2 * pair + 1])
        live_chunks = (longest[pair] + CHUNK - 1) // CHUNK

        def score(chunk, peak):
            start = pl.multiple_of(chunk * CHUNK, CHUNK)
            block = lax.dot_general(
                q_wide, wide(keys, pair, start), (((1,), (1,)), ((), ())), preferred_element_type=F32
            )
            slot = lax.broadcasted_iota(jnp.int32, (2 * QG, CHUNK), 1) + start
            block = jnp.where(slot < length, block * scale, -1e30)
            scores[:, pl.ds(start, CHUNK)] = block
            for t in range(CHUNK // HD):
                peak = jnp.maximum(peak, block[:, t * HD : (t + 1) * HD])
            return peak

        peak = lax.fori_loop(0, live_chunks, score, jnp.full((2 * QG, HD), -1e30, F32))
        peak = jnp.maximum(jnp.max(peak, axis=1, keepdims=True), fresh)

        def mix(chunk, carry):
            mass, mixed = carry
            start = pl.multiple_of(chunk * CHUNK, CHUNK)
            weight = jnp.exp(scores[:, pl.ds(start, CHUNK)] - peak)
            for t in range(CHUNK // HD):
                mass = mass + weight[:, t * HD : (t + 1) * HD]
            mixed = mixed + jnp.dot(
                weight.astype(BF16), wide(values, pair, start), preferred_element_type=F32
            )
            return mass, mixed

        mass, mixed = lax.fori_loop(
            0, live_chunks, mix, (jnp.zeros((2 * QG, HD), F32), jnp.zeros((2 * QG, 2 * HD), F32))
        )
        weight_new = jnp.exp(fresh - peak)
        denominator = jnp.sum(mass, axis=1, keepdims=True) + weight_new
        own = jnp.concatenate([mixed[:QG, :HD], mixed[QG:, HD:]], axis=0)
        own = (own + weight_new.astype(BF16).astype(F32) * v_new) / denominator
        attended[2 * QG * pair : 2 * QG * (pair + 1), :] = own

    matrix = hadamard_signs()
    steered = []
    for h in range(QG):
        steered.append(attended[pl.ds(h, lists, stride=QG), :] * sign_ref[:, h * HD : (h + 1) * HD])
    turned = two_piece_dot(jnp.concatenate(steered, axis=0), matrix) * (1.0 / math.sqrt(HD))
    for h in range(QG):
        piece = turned[lists * h : lists * (h + 1)].astype(BF16)
        for w in range(out_ref.shape[0]):
            out_ref[w, :, h * HD : (h + 1) * HD] = piece


def mix_kernel(place_ref, rows_ref, weight, keep_ref, send_ref):
    parts, width = 4, weight.shape[1] // 4
    c = place_ref[1]
    rows = jnp.concatenate([rows_ref[x, c] for x in range(4)] + [rows_ref[x, 1 - c] for x in range(4)], axis=0)
    for i in range(parts):
        product = jnp.dot(rows, weight[:, i * width : (i + 1) * width], preferred_element_type=F32)
        for x in range(4):
            keep_ref[x, :, i * width : (i + 1) * width] = product[16 * x : 16 * x + 16]
            send_ref[x, :, i * width : (i + 1) * width] = product[64 + 16 * x : 80 + 16 * x].astype(BF16)


def pair_sum_kernel(place_ref, keep_ref, got_ref, own_ref, s1, s2, s3):
    x = place_ref[0]
    own_ref[...] = keep_ref[x] + got_ref[x].astype(F32)
    for s, ref in ((1, s1), (2, s2), (3, s3)):
        to = (x + s) & 3
        ref[...] = (keep_ref[to] + got_ref[to].astype(F32)).astype(BF16)


def last_kernel(hidden_ref, own_ref, r1, r2, r3, out_ref):
    mixed = own_ref[...] + r1[...].astype(F32) + r2[...].astype(F32) + r3[...].astype(F32)
    out_ref[...] = (hidden_ref[...].astype(F32) + mixed).astype(BF16)


def params(limit):
    return pltpu.CompilerParams(vmem_limit_bytes=limit * MIB)


def cost(microseconds):
    return pl.CostEstimate(flops=int(microseconds * 1.1e9), transcendentals=0, bytes_accessed=int(microseconds * 3e6))


def along_x(value):
    return [lax.ppermute(value, "x", [(i, (i + s) % 4) for i in range(4)]) for s in (1, 2, 3)]


def across_cores(value):
    return lax.ppermute(value, "core", [(0, 1), (1, 0)])


def body(hidden, gain, sign_in, qkv_weight, out_weight, sign_attn, key_cache, value_cache, lengths):
    rows, features = hidden.shape
    columns = qkv_weight.shape[1]
    own_lists, _, slots, _ = key_cache.shape
    peers = lax.axis_size(WIDE)
    place = jnp.stack([lax.axis_index("x"), lax.axis_index("core")]).astype(jnp.int32)

    steer = gain.astype(F32) * (2 * sign_in - 1).astype(F32)
    rotated = pl.pallas_call(
        rotate_in_kernel,
        out_shape=jax.ShapeDtypeStruct((2 * rows, features + EXTRA), BF16),
        in_specs=[VMEM] * 3,
        out_specs=VMEM,
        compiler_params=params(4),
        cost_estimate=cost(COVER[0]),
        name="rotate_in",
    )(hidden, across_cores(hidden), steer.reshape(1, -1))
    partial = pl.pallas_call(
        project_kernel,
        out_shape=jax.ShapeDtypeStruct((peers, own_lists, columns + EXTRA), BF16),
        in_specs=[SMEM] + [VMEM] * 5,
        out_specs=VMEM,
        compiler_params=params(8),
        cost_estimate=cost(COVER[1]),
        name="project",
    )(place, rotated, *along_x(rotated), qkv_weight)
    arrived = lax.all_to_all(partial, WIDE, split_axis=0, concat_axis=0, tiled=True)

    frequency = jnp.exp(jnp.arange(HD // 2, dtype=F32) * (-2.0 * math.log(ROPE_BASE) / HD))
    angles = lengths.astype(F32)[:, None] * frequency[None, :]
    cosine, sine = jnp.cos(angles), jnp.sin(angles)
    sent = pl.pallas_call(
        attend_kernel,
        out_shape=jax.ShapeDtypeStruct((peers, own_lists, QG * HD), BF16),
        in_specs=[SMEM] + [VMEM] * 6,
        out_specs=VMEM,
        scratch_shapes=[
            pltpu.VMEM((own_lists, 24, HD), F32),
            pltpu.VMEM((2 * QG, slots), F32),
            pltpu.VMEM((own_lists * QG, HD), F32),
        ],
        compiler_params=params(20),
        cost_estimate=cost(COVER[2]),
        name="attend",
    )(
        jnp.minimum(lengths, slots),
        arrived,
        jnp.concatenate([cosine, cosine], axis=1),
        jnp.concatenate([-sine, sine], axis=1),
        (2 * sign_attn - 1).astype(F32).reshape(1, -1),
        key_cache,
        value_cache,
    )
    gathered = lax.all_to_all(sent, WIDE, split_axis=0, concat_axis=0, tiled=True)
    keep, send = pl.pallas_call(
        mix_kernel,
        out_shape=(
            jax.ShapeDtypeStruct((4, rows, features), F32),
            jax.ShapeDtypeStruct((4, rows, features), BF16),
        ),
        in_specs=[SMEM, VMEM, VMEM],
        out_specs=(VMEM, VMEM),
        compiler_params=params(8),
        name="mix",
    )(place, gathered.reshape(4, 2, rows, QG * HD), out_weight)
    own, *sends = pl.pallas_call(
        pair_sum_kernel,
        out_shape=(jax.ShapeDtypeStruct((rows, features), F32),)
        + (jax.ShapeDtypeStruct((rows, features), BF16),) * 3,
        in_specs=[SMEM, VMEM, VMEM],
        out_specs=(VMEM,) * 4,
        compiler_params=params(4),
        name="pair_sum",
    )(place, keep, across_cores(send))
    got = [
        lax.ppermute(v, "x", [(i, (i + s) % 4) for i in range(4)]) for s, v in zip((1, 2, 3), sends)
    ]
    return pl.pallas_call(
        last_kernel,
        out_shape=jax.ShapeDtypeStruct((rows, features), BF16),
        in_specs=[VMEM] * 5,
        out_specs=VMEM,
        compiler_params=params(4),
        name="last",
    )(hidden, own, *got)


def solution(mesh):
    split = Mesh(mesh.devices.reshape(4, 4, 4, 2), ("y", "z", "x", "core"))
    narrow = ("x", "core")
    placed = (
        P(narrow, WIDE),
        P(WIDE),
        P(WIDE),
        P(WIDE, narrow),
        P(narrow, WIDE),
        P(narrow),
        P(WIDE, narrow, None, None),
        P(WIDE, narrow, None, None),
        P(WIDE),
    )
    return jax.shard_map(
        body, mesh=split, in_specs=placed, out_specs=P(narrow, WIDE), check_vma=False
    )
```

```python
import math

import jax
import jax.numpy as jnp
from jax import lax
from jax.experimental import pallas as pl
from jax.experimental.pallas import tpu as pltpu
from jax.sharding import Mesh
from jax.sharding import PartitionSpec as P

D = 16384
HD = 128
QG = 16
WIDE = ("y", "z")
ROPE_BASE = 500000.0
EXTRA = 128
MIB = 1 << 20
VMEM = pl.BlockSpec(memory_space=pltpu.VMEM)
SMEM = pl.BlockSpec(memory_space=pltpu.SMEM)
HBM = pl.BlockSpec(memory_space=pl.ANY)
F32 = jnp.float32
BF16 = jnp.bfloat16


def hadamard_signs():
    common = lax.broadcasted_iota(jnp.int32, (HD, HD), 0) & lax.broadcasted_iota(jnp.int32, (HD, HD), 1)
    common = common ^ (common >> 4)
    common = common ^ (common >> 2)
    common = common ^ (common >> 1)
    return (1 - 2 * (common & 1)).astype(F32).astype(BF16)


def two_piece_dot(values, matrix):
    high = values.astype(BF16)
    low = (values - high.astype(F32)).astype(BF16)
    return jnp.dot(high, matrix, preferred_element_type=F32) + jnp.dot(low, matrix, preferred_element_type=F32)


def rotate_in_kernel(own_ref, other_ref, steer_ref, out_ref):
    features = own_ref.shape[1]
    matrix = hadamard_signs()
    steer = steer_ref[...]
    lane = lax.broadcasted_iota(jnp.int32, (16, EXTRA), 1)
    for at, ref in enumerate((own_ref, other_ref)):
        rows = ref[...].astype(F32)
        squares = jnp.sum(rows * rows, axis=1, keepdims=True)
        first = squares.astype(BF16).astype(F32)
        second = (squares - first).astype(BF16).astype(F32)
        third = squares - first - second
        pieces = jnp.where(lane == 0, first, jnp.where(lane == 1, second, jnp.where(lane == 2, third, 0.0)))
        out_ref[16 * at : 16 * at + 16, features:] = pieces.astype(BF16)
        steered = rows * steer
        for b in range(features // HD):
            turned = two_piece_dot(steered[:, b * HD : (b + 1) * HD], matrix) * (1.0 / math.sqrt(HD))
            out_ref[16 * at : 16 * at + 16, b * HD : (b + 1) * HD] = turned.astype(BF16)


def project_kernel(place_ref, x0, x1, x2, x3, weight, out_ref):
    parts, width = 3, weight.shape[1] // 3
    features = weight.shape[0]
    x, c = place_ref[0], place_ref[1]
    received = (x0, x1, x2, x3)
    targets = []
    for s in range(4):
        for other in range(2):
            core = c if other == 0 else 1 - c
            source = 2 * ((x - s) & 3) + core
            targets += [2 * source, 2 * source + 1]
    for s in range(4):
        extra = received[s][:, features:].astype(F32)
        for j in range(4):
            out_ref[targets[4 * s + j], :, weight.shape[1] :] = extra[8 * j : 8 * j + 8].astype(BF16)
    rows = jnp.concatenate([r[:, :features] for r in received], axis=0)
    for i in range(parts):
        product = jnp.dot(rows, weight[:, i * width : (i + 1) * width], preferred_element_type=F32)
        for j in range(16):
            out_ref[targets[j], :, i * width : (i + 1) * width] = product[8 * j : 8 * j + 8].astype(BF16)


COVER = (10, 10, 10)
TILE = 512


def attend_kernel(
    lengths_ref, arrived_ref, cos_ref, sin_ref, sign_ref, keys, values, out_ref, queries, scores, attended
):
    lists, slots = keys.shape[0], keys.shape[2]
    pairs = lists // 2

    def wide(ref, pair, start):
        span = slice(start, start + TILE)
        return jnp.concatenate([ref[2 * pair, 0, span, :], ref[2 * pair + 1, 0, span, :]], axis=1)

    total = arrived_ref[0].astype(F32)
    for w in range(1, arrived_ref.shape[0]):
        total = total + arrived_ref[w].astype(F32)
    columns = (QG + 2) * HD
    squares = jnp.sum(total[:, columns:], axis=1, keepdims=True)
    factor = lax.rsqrt(squares * (1.0 / D) + 1e-05)
    cosine, sine = cos_ref[...], sin_ref[...]
    for h in range(QG + 2):
        vector = total[:, h * HD : (h + 1) * HD] * factor
        if h <= QG:
            vector = vector * cosine + pltpu.roll(vector, HD // 2, 1) * sine
        queries[:, h, :] = vector.astype(BF16).astype(F32)

    scale = math.log2(math.e) / math.sqrt(HD)
    row = lax.broadcasted_iota(jnp.int32, (2 * QG, 1), 0)

    def score(pair):
        first, second = queries[2 * pair], queries[2 * pair + 1]
        q_both = jnp.concatenate([first[:QG], second[:QG]], axis=0)
        blank = jnp.zeros((QG, HD), F32)
        q_wide = jnp.concatenate(
            [jnp.concatenate([first[:QG], blank], axis=1), jnp.concatenate([blank, second[:QG]], axis=1)], axis=0
        ).astype(BF16)
        k_new = jnp.concatenate([jnp.broadcast_to(v[QG : QG + 1], (QG, HD)) for v in (first, second)], axis=0)
        fresh = jnp.sum(q_both * k_new, axis=1, keepdims=True) * scale
        length = jnp.where(row < QG, lengths_ref[2 * pair], lengths_ref[2 * pair + 1])
        peak = jnp.full((2 * QG, HD), -1e30, F32)
        for start in range(0, slots, TILE):
            block = lax.dot_general(
                q_wide, wide(keys, pair, start), (((1,), (1,)), ((), ())), preferred_element_type=F32
            )
            slot = lax.broadcasted_iota(jnp.int32, (2 * QG, TILE), 1) + start
            block = jnp.where(slot < length, block * scale, -1e30)
            scores[pair, :, start : start + TILE] = block
            for t in range(TILE // HD):
                peak = jnp.maximum(peak, block[:, t * HD : (t + 1) * HD])
        return fresh, jnp.maximum(jnp.max(peak, axis=1, keepdims=True), fresh)

    def mix(pair, fresh, peak):
        mass = jnp.zeros((2 * QG, HD), F32)
        mixed = jnp.zeros((2 * QG, 2 * HD), F32)
        for start in range(0, slots, TILE):
            weight = jnp.exp2(scores[pair, :, start : start + TILE] - peak)
            for t in range(TILE // HD):
                mass = mass + weight[:, t * HD : (t + 1) * HD]
            mixed = mixed + jnp.dot(weight.astype(BF16), wide(values, pair, start), preferred_element_type=F32)
        weight_new = jnp.exp2(fresh - peak)
        denominator = jnp.sum(mass, axis=1, keepdims=True) + weight_new
        v_new = jnp.concatenate(
            [jnp.broadcast_to(queries[2 * pair + j, QG + 1 : QG + 2, :], (QG, HD)) for j in range(2)], axis=0
        )
        own = jnp.concatenate([mixed[:QG, :HD], mixed[QG:, HD:]], axis=0)
        own = (own + weight_new.astype(BF16).astype(F32) * v_new) / denominator
        attended[2 * QG * pair : 2 * QG * (pair + 1), :] = own

    ahead = score(0)
    for pair in range(pairs):
        this, ahead = ahead, score(pair + 1) if pair + 1 < pairs else None
        mix(pair, *this)

    matrix = hadamard_signs()
    steered = []
    for h in range(QG):
        steered.append(attended[pl.ds(h, lists, stride=QG), :] * sign_ref[:, h * HD : (h + 1) * HD])
    turned = two_piece_dot(jnp.concatenate(steered, axis=0), matrix) * (1.0 / math.sqrt(HD))
    for h in range(QG):
        piece = turned[lists * h : lists * (h + 1)].astype(BF16)
        for w in range(out_ref.shape[0]):
            out_ref[w, :, h * HD : (h + 1) * HD] = piece


def mix_kernel(place_ref, rows_ref, weight, keep_ref, send_ref):
    parts, width = 4, weight.shape[1] // 4
    c = place_ref[1]
    rows = jnp.concatenate([rows_ref[x, c] for x in range(4)] + [rows_ref[x, 1 - c] for x in range(4)], axis=0)
    for i in range(parts):
        product = jnp.dot(rows, weight[:, i * width : (i + 1) * width], preferred_element_type=F32)
        for x in range(4):
            keep_ref[x, :, i * width : (i + 1) * width] = product[16 * x : 16 * x + 16]
            send_ref[x, :, i * width : (i + 1) * width] = product[64 + 16 * x : 80 + 16 * x].astype(BF16)


def pair_sum_kernel(place_ref, keep_ref, got_ref, own_ref, s1, s2, s3):
    x = place_ref[0]
    own_ref[...] = keep_ref[x] + got_ref[x].astype(F32)
    for s, ref in ((1, s1), (2, s2), (3, s3)):
        to = (x + s) & 3
        ref[...] = (keep_ref[to] + got_ref[to].astype(F32)).astype(BF16)


def last_kernel(hidden_ref, own_ref, r1, r2, r3, out_ref):
    mixed = own_ref[...] + r1[...].astype(F32) + r2[...].astype(F32) + r3[...].astype(F32)
    out_ref[...] = (hidden_ref[...].astype(F32) + mixed).astype(BF16)


def params(limit):
    return pltpu.CompilerParams(vmem_limit_bytes=limit * MIB)


def cost(microseconds):
    return pl.CostEstimate(flops=int(microseconds * 1.1e9), transcendentals=0, bytes_accessed=int(microseconds * 3e6))


def along_x(value):
    return [lax.ppermute(value, "x", [(i, (i + s) % 4) for i in range(4)]) for s in (1, 2, 3)]


def across_cores(value):
    return lax.ppermute(value, "core", [(0, 1), (1, 0)])


def body(hidden, gain, sign_in, qkv_weight, out_weight, sign_attn, key_cache, value_cache, lengths):
    rows, features = hidden.shape
    columns = qkv_weight.shape[1]
    own_lists, _, slots, _ = key_cache.shape
    peers = lax.axis_size(WIDE)
    place = jnp.stack([lax.axis_index("x"), lax.axis_index("core")]).astype(jnp.int32)

    steer = gain.astype(F32) * (2 * sign_in - 1).astype(F32)
    rotated = pl.pallas_call(
        rotate_in_kernel,
        out_shape=jax.ShapeDtypeStruct((2 * rows, features + EXTRA), BF16),
        in_specs=[VMEM] * 3,
        out_specs=VMEM,
        compiler_params=params(2),
        cost_estimate=cost(COVER[0]),
        name="rotate_in",
    )(hidden.astype(F32), across_cores(hidden), steer.reshape(1, -1))
    rotated, lengths, sign_attn = lax.optimization_barrier((rotated, lengths, sign_attn))
    frequency = jnp.exp(jnp.arange(HD // 2, dtype=F32) * (-2.0 * math.log(ROPE_BASE) / HD))
    angles = lengths.astype(F32)[:, None] * frequency[None, :]
    cosine, sine = jnp.cos(angles), jnp.sin(angles)
    cosine = jnp.concatenate([cosine, cosine], axis=1)
    sine = jnp.concatenate([-sine, sine], axis=1)
    sign_out = (2 * sign_attn - 1).astype(F32).reshape(1, -1)
    received = along_x(rotated)
    received, cosine, sine, sign_out, lengths = lax.optimization_barrier((received, cosine, sine, sign_out, jnp.minimum(lengths, slots)))
    partial = pl.pallas_call(
        project_kernel,
        out_shape=jax.ShapeDtypeStruct((peers, own_lists, columns + EXTRA), BF16),
        in_specs=[SMEM] + [VMEM] * 5,
        out_specs=VMEM,
        compiler_params=params(2),
        cost_estimate=cost(COVER[1]),
        name="project",
    )(place, rotated, *received, qkv_weight)
    arrived = lax.all_to_all(partial, WIDE, split_axis=0, concat_axis=0, tiled=True)

    sent = pl.pallas_call(
        attend_kernel,
        out_shape=jax.ShapeDtypeStruct((peers, own_lists, QG * HD), BF16),
        in_specs=[SMEM] + [VMEM] * 6,
        out_specs=VMEM,
        scratch_shapes=[
            pltpu.VMEM((own_lists, 24, HD), F32),
            pltpu.VMEM((own_lists // 2, 2 * QG, slots), F32),
            pltpu.VMEM((own_lists * QG, HD), F32),
        ],
        compiler_params=params(6),
        cost_estimate=cost(COVER[2]),
        name="attend",
    )(
        lengths,
        arrived,
        cosine,
        sine,
        sign_out,
        key_cache,
        value_cache,
    )
    gathered = lax.all_to_all(sent, WIDE, split_axis=0, concat_axis=0, tiled=True)
    keep, send = pl.pallas_call(
        mix_kernel,
        out_shape=(
            jax.ShapeDtypeStruct((4, rows, features), F32),
            jax.ShapeDtypeStruct((4, rows, features), BF16),
        ),
        in_specs=[SMEM, VMEM, VMEM],
        out_specs=(VMEM, VMEM),
        compiler_params=params(2),
        name="mix",
    )(place, gathered.reshape(4, 2, rows, QG * HD), out_weight)
    own, *sends = pl.pallas_call(
        pair_sum_kernel,
        out_shape=(jax.ShapeDtypeStruct((rows, features), F32),)
        + (jax.ShapeDtypeStruct((rows, features), BF16),) * 3,
        in_specs=[SMEM, VMEM, VMEM],
        out_specs=(VMEM,) * 4,
        compiler_params=params(2),
        name="pair_sum",
    )(place, keep, across_cores(send))
    got = [
        lax.ppermute(v, "x", [(i, (i + s) % 4) for i in range(4)]) for s, v in zip((1, 2, 3), sends)
    ]
    return pl.pallas_call(
        last_kernel,
        out_shape=jax.ShapeDtypeStruct((rows, features), BF16),
        in_specs=[VMEM] * 5,
        out_specs=VMEM,
        compiler_params=params(2),
        name="last",
    )(hidden, own, *got)


def solution(mesh):
    split = Mesh(mesh.devices.reshape(4, 4, 4, 2), ("y", "z", "x", "core"))
    narrow = ("x", "core")
    placed = (
        P(narrow, WIDE),
        P(WIDE),
        P(WIDE),
        P(WIDE, narrow),
        P(narrow, WIDE),
        P(narrow),
        P(WIDE, narrow, None, None),
        P(WIDE, narrow, None, None),
        P(WIDE),
    )
    return jax.shard_map(
        body, mesh=split, in_specs=placed, out_specs=P(narrow, WIDE), check_vma=False
    )
```

```python
import math

import jax
import jax.numpy as jnp
from jax import lax
from jax.experimental import pallas as pl
from jax.experimental.pallas import tpu as pltpu
from jax.sharding import Mesh
from jax.sharding import PartitionSpec as P

D = 16384
HD = 128
QG = 16
WIDE = ("y", "z")
ROPE_BASE = 500000.0
EXTRA = 128
MIB = 1 << 20
VMEM = pl.BlockSpec(memory_space=pltpu.VMEM)
HBM = pl.BlockSpec(memory_space=pl.ANY)
F32 = jnp.float32
BF16 = jnp.bfloat16


def hadamard_signs():
    common = lax.broadcasted_iota(jnp.int32, (HD, HD), 0) & lax.broadcasted_iota(jnp.int32, (HD, HD), 1)
    common = common ^ (common >> 4)
    common = common ^ (common >> 2)
    common = common ^ (common >> 1)
    return (1 - 2 * (common & 1)).astype(F32).astype(BF16)


def two_piece_dot(values, matrix):
    high = values.astype(BF16)
    low = (values - high.astype(F32)).astype(BF16)
    return jnp.dot(high, matrix, preferred_element_type=F32) + jnp.dot(low, matrix, preferred_element_type=F32)


def rotate_in_kernel(own_ref, other_ref, steer_ref, out_ref):
    features = own_ref.shape[1]
    matrix = hadamard_signs()
    steer = steer_ref[...]
    lane = lax.broadcasted_iota(jnp.int32, (16, EXTRA), 1)
    for at, ref in enumerate((own_ref, other_ref)):
        rows = ref[...].astype(F32)
        squares = jnp.sum(rows * rows, axis=1, keepdims=True)
        first = squares.astype(BF16).astype(F32)
        second = (squares - first).astype(BF16).astype(F32)
        third = squares - first - second
        pieces = jnp.where(lane == 0, first, jnp.where(lane == 1, second, jnp.where(lane == 2, third, 0.0)))
        out_ref[16 * at : 16 * at + 16, features:] = pieces.astype(BF16)
        steered = rows * steer
        for b in range(features // HD):
            turned = two_piece_dot(steered[:, b * HD : (b + 1) * HD], matrix) * (1.0 / math.sqrt(HD))
            out_ref[16 * at : 16 * at + 16, b * HD : (b + 1) * HD] = turned.astype(BF16)


def project_kernel(x0, x1, x2, x3, weight, out_ref):
    parts, width = 3, weight.shape[1] // 3
    features = weight.shape[0]
    x, c = lax.axis_index("x"), lax.axis_index("core")
    received = (x0, x1, x2, x3)
    targets = []
    for s in range(4):
        for other in range(2):
            core = c if other == 0 else 1 - c
            source = 2 * (x ^ s) + core
            targets += [2 * source, 2 * source + 1]
    for s in range(4):
        extra = received[s][:, features:].astype(F32)
        for j in range(4):
            out_ref[targets[4 * s + j], :, weight.shape[1] :] = extra[8 * j : 8 * j + 8].astype(BF16)
    rows = jnp.concatenate([r[:, :features] for r in received], axis=0)
    for i in range(parts):
        product = jnp.dot(rows, weight[:, i * width : (i + 1) * width], preferred_element_type=F32)
        for j in range(16):
            out_ref[targets[j], :, i * width : (i + 1) * width] = product[8 * j : 8 * j + 8].astype(BF16)


COVER = (30, 1, 10)
TILE = 512


def attend_kernel(
    lengths_ref, arrived_ref, cos_ref, sin_ref, sign_ref, keys, values, out_ref, queries, scores, attended
):
    lists, slots = keys.shape[0], keys.shape[2]
    pairs = lists // 2

    def wide(ref, pair, start):
        span = slice(start, start + TILE)
        return jnp.concatenate([ref[2 * pair, 0, span, :], ref[2 * pair + 1, 0, span, :]], axis=1)

    total = arrived_ref[0].astype(F32)
    for w in range(1, arrived_ref.shape[0]):
        total = total + arrived_ref[w].astype(F32)
    columns = (QG + 2) * HD
    squares = jnp.sum(total[:, columns:], axis=1, keepdims=True)
    factor = lax.rsqrt(squares * (1.0 / D) + 1e-05)
    cosine, sine = cos_ref[...], sin_ref[...]
    for h in range(QG + 2):
        vector = total[:, h * HD : (h + 1) * HD] * factor
        if h <= QG:
            vector = vector * cosine + pltpu.roll(vector, HD // 2, 1) * sine
        queries[:, h, :] = vector.astype(BF16).astype(F32)

    scale = math.log2(math.e) / math.sqrt(HD)
    lane = lax.broadcasted_iota(jnp.int32, (2 * QG, HD), 1)

    def score(pair):
        first, second = queries[2 * pair], queries[2 * pair + 1]
        q_both = jnp.concatenate([first[:QG], second[:QG]], axis=0)
        blank = jnp.zeros((QG, HD), F32)
        q_wide = jnp.concatenate(
            [jnp.concatenate([first[:QG], blank], axis=1), jnp.concatenate([blank, second[:QG]], axis=1)], axis=0
        ).astype(BF16)
        k_new = jnp.concatenate([jnp.broadcast_to(v[QG : QG + 1], (QG, HD)) for v in (first, second)], axis=0)
        fresh = jnp.sum(q_both * k_new, axis=1, keepdims=True) * scale
        length = jnp.concatenate(
            [jnp.broadcast_to(lengths_ref[2 * pair + j : 2 * pair + j + 1, :], (QG, HD)) for j in range(2)], axis=0
        )
        peak = jnp.full((2 * QG, HD), -1e30, F32)
        for start in range(0, slots, TILE):
            block = lax.dot_general(
                q_wide, wide(keys, pair, start), (((1,), (1,)), ((), ())), preferred_element_type=F32
            )
            for t in range(TILE // HD):
                at = start + t * HD
                piece = jnp.where(lane < length - at, block[:, t * HD : (t + 1) * HD] * scale, -1e30)
                scores[pair, :, at : at + HD] = piece
                peak = jnp.maximum(peak, piece)
        return fresh, jnp.maximum(jnp.max(peak, axis=1, keepdims=True), fresh)

    def mix(pair, fresh, peak):
        mass = jnp.zeros((2 * QG, HD), F32)
        mixed = jnp.zeros((2 * QG, 2 * HD), F32)
        for start in range(0, slots, TILE):
            weight = jnp.exp2(scores[pair, :, start : start + TILE] - peak)
            for t in range(TILE // HD):
                mass = mass + weight[:, t * HD : (t + 1) * HD]
            mixed = mixed + jnp.dot(weight.astype(BF16), wide(values, pair, start), preferred_element_type=F32)
        weight_new = jnp.exp2(fresh - peak)
        denominator = jnp.sum(mass, axis=1, keepdims=True) + weight_new
        v_new = jnp.concatenate(
            [jnp.broadcast_to(queries[2 * pair + j, QG + 1 : QG + 2, :], (QG, HD)) for j in range(2)], axis=0
        )
        own = jnp.concatenate([mixed[:QG, :HD], mixed[QG:, HD:]], axis=0)
        own = (own + weight_new.astype(BF16).astype(F32) * v_new) / denominator
        attended[2 * QG * pair : 2 * QG * (pair + 1), :] = own

    ahead = score(0)
    for pair in range(pairs):
        this, ahead = ahead, score(pair + 1) if pair + 1 < pairs else None
        mix(pair, *this)

    matrix = hadamard_signs()
    steered = []
    for h in range(QG):
        steered.append(attended[pl.ds(h, lists, stride=QG), :] * sign_ref[:, h * HD : (h + 1) * HD])
    turned = two_piece_dot(jnp.concatenate(steered, axis=0), matrix) * (1.0 / math.sqrt(HD))
    for h in range(QG):
        piece = turned[lists * h : lists * (h + 1)].astype(BF16)
        for w in range(out_ref.shape[0]):
            out_ref[w, :, h * HD : (h + 1) * HD] = piece


def mix_kernel(rows_ref, weight, keep_ref, send_ref):
    parts, width = 4, weight.shape[1] // 4
    c = lax.axis_index("core")
    rows = jnp.concatenate([rows_ref[x, c] for x in range(4)] + [rows_ref[x, 1 - c] for x in range(4)], axis=0)
    for i in range(parts):
        product = jnp.dot(rows, weight[:, i * width : (i + 1) * width], preferred_element_type=F32)
        for x in range(4):
            keep_ref[x, :, i * width : (i + 1) * width] = product[16 * x : 16 * x + 16]
            send_ref[x, :, i * width : (i + 1) * width] = product[64 + 16 * x : 80 + 16 * x].astype(BF16)


def pair_sum_kernel(keep_ref, got_ref, own_ref, s1, s2, s3):
    x = lax.axis_index("x")
    own_ref[...] = keep_ref[x] + got_ref[x].astype(F32)
    for s, ref in ((1, s1), (2, s2), (3, s3)):
        to = x ^ s
        ref[...] = (keep_ref[to] + got_ref[to].astype(F32)).astype(BF16)


def last_kernel(hidden_ref, own_ref, r1, r2, r3, out_ref):
    mixed = own_ref[...] + r1[...].astype(F32) + r2[...].astype(F32) + r3[...].astype(F32)
    out_ref[...] = (hidden_ref[...].astype(F32) + mixed).astype(BF16)


def params(limit):
    return pltpu.CompilerParams(vmem_limit_bytes=limit * MIB)


def cost(microseconds):
    return pl.CostEstimate(flops=int(microseconds * 1.1e9), transcendentals=0, bytes_accessed=int(microseconds * 3e6))


def along_x(values):
    return [lax.ppermute(v, "x", [(i, i ^ s) for i in range(4)]) for s, v in zip((1, 2, 3), values)]


def across_cores(value):
    return lax.ppermute(value, "core", [(0, 1), (1, 0)])


def body(hidden, gain, sign_in, qkv_weight, out_weight, sign_attn, key_cache, value_cache, lengths):
    rows, features = hidden.shape
    columns = qkv_weight.shape[1]
    own_lists, _, slots, _ = key_cache.shape
    peers = lax.axis_size(WIDE)

    steer = gain.astype(F32) * (2 * sign_in - 1).astype(F32)
    rotated = pl.pallas_call(
        rotate_in_kernel,
        out_shape=jax.ShapeDtypeStruct((2 * rows, features + EXTRA), BF16),
        in_specs=[VMEM] * 3,
        out_specs=VMEM,
        compiler_params=params(2),
        cost_estimate=cost(COVER[0]),
        name="rotate_in",
    )(hidden.astype(F32), across_cores(hidden), steer.reshape(1, -1))
    rotated, lengths, sign_attn = lax.optimization_barrier((rotated, lengths, sign_attn))
    frequency = jnp.exp(jnp.arange(HD // 2, dtype=F32) * (-2.0 * math.log(ROPE_BASE) / HD))
    angles = lengths.astype(F32)[:, None] * frequency[None, :]
    cosine, sine = jnp.cos(angles), jnp.sin(angles)
    cosine = jnp.concatenate([cosine, cosine], axis=1)
    sine = jnp.concatenate([-sine, sine], axis=1)
    sign_out = (2 * sign_attn - 1).astype(F32).reshape(1, -1)
    received = along_x([rotated] * 3)
    received, cosine, sine, sign_out, lengths = lax.optimization_barrier((received, cosine, sine, sign_out, jnp.broadcast_to(lengths[:, None], (own_lists, HD))))
    partial = pl.pallas_call(
        project_kernel,
        out_shape=jax.ShapeDtypeStruct((peers, own_lists, columns + EXTRA), BF16),
        in_specs=[VMEM] * 5,
        out_specs=VMEM,
        compiler_params=params(2),
        cost_estimate=cost(COVER[1]),
        name="project",
    )(rotated, *received, qkv_weight)
    arrived = lax.all_to_all(partial, WIDE, split_axis=0, concat_axis=0, tiled=True)

    sent = pl.pallas_call(
        attend_kernel,
        out_shape=jax.ShapeDtypeStruct((peers, own_lists, QG * HD), BF16),
        in_specs=[VMEM] * 7,
        out_specs=VMEM,
        scratch_shapes=[
            pltpu.VMEM((own_lists, 24, HD), F32),
            pltpu.VMEM((own_lists // 2, 2 * QG, slots), F32),
            pltpu.VMEM((own_lists * QG, HD), F32),
        ],
        compiler_params=params(6),
        cost_estimate=cost(COVER[2]),
        name="attend",
    )(
        lengths,
        arrived,
        cosine,
        sine,
        sign_out,
        key_cache,
        value_cache,
    )
    gathered = lax.all_to_all(sent, WIDE, split_axis=0, concat_axis=0, tiled=True)
    keep, send = pl.pallas_call(
        mix_kernel,
        out_shape=(
            jax.ShapeDtypeStruct((4, rows, features), F32),
            jax.ShapeDtypeStruct((4, rows, features), BF16),
        ),
        in_specs=[VMEM, VMEM],
        out_specs=(VMEM, VMEM),
        compiler_params=params(2),
        name="mix",
    )(gathered.reshape(4, 2, rows, QG * HD), out_weight)
    own, *sends = pl.pallas_call(
        pair_sum_kernel,
        out_shape=(jax.ShapeDtypeStruct((rows, features), F32),)
        + (jax.ShapeDtypeStruct((rows, features), BF16),) * 3,
        in_specs=[VMEM, VMEM],
        out_specs=(VMEM,) * 4,
        compiler_params=params(2),
        name="pair_sum",
    )(keep, across_cores(send))
    got = along_x(sends)
    return pl.pallas_call(
        last_kernel,
        out_shape=jax.ShapeDtypeStruct((rows, features), BF16),
        in_specs=[VMEM] * 5,
        out_specs=VMEM,
        compiler_params=params(2),
        name="last",
    )(hidden, own, *got)


def solution(mesh):
    split = Mesh(mesh.devices.reshape(4, 4, 4, 2), ("y", "z", "x", "core"))
    narrow = ("x", "core")
    placed = (
        P(narrow, WIDE),
        P(WIDE),
        P(WIDE),
        P(WIDE, narrow),
        P(narrow, WIDE),
        P(narrow),
        P(WIDE, narrow, None, None),
        P(WIDE, narrow, None, None),
        P(WIDE),
    )
    return jax.shard_map(
        body, mesh=split, in_specs=placed, out_specs=P(narrow, WIDE), check_vma=False
    )
```

```python
import math

import jax
import jax.numpy as jnp
from jax import lax
from jax.experimental import pallas as pl
from jax.experimental.pallas import tpu as pltpu
from jax.sharding import Mesh
from jax.sharding import PartitionSpec as P

D = 16384
HD = 128
QG = 16
WIDE = ("y", "z")
ROPE_BASE = 500000.0
EXTRA = 128
MIB = 1 << 20
VMEM = pl.BlockSpec(memory_space=pltpu.VMEM)
HBM = pl.BlockSpec(memory_space=pl.ANY)
F32 = jnp.float32
BF16 = jnp.bfloat16


def hadamard_signs():
    common = lax.broadcasted_iota(jnp.int32, (HD, HD), 0) & lax.broadcasted_iota(jnp.int32, (HD, HD), 1)
    common = common ^ (common >> 4)
    common = common ^ (common >> 2)
    common = common ^ (common >> 1)
    return (1 - 2 * (common & 1)).astype(F32).astype(BF16)


def two_piece_dot(values, matrix):
    high = values.astype(BF16)
    low = (values - high.astype(F32)).astype(BF16)
    return jnp.dot(high, matrix, preferred_element_type=F32) + jnp.dot(low, matrix, preferred_element_type=F32)


def rotate_in_kernel(own_ref, other_ref, steer_ref, out_ref):
    features = own_ref.shape[1]
    matrix = hadamard_signs()
    steer = steer_ref[...]
    lane = lax.broadcasted_iota(jnp.int32, (16, EXTRA), 1)
    for at, ref in enumerate((own_ref, other_ref)):
        rows = ref[...].astype(F32)
        squares = jnp.sum(rows * rows, axis=1, keepdims=True)
        first = squares.astype(BF16).astype(F32)
        second = (squares - first).astype(BF16).astype(F32)
        third = squares - first - second
        pieces = jnp.where(lane == 0, first, jnp.where(lane == 1, second, jnp.where(lane == 2, third, 0.0)))
        out_ref[16 * at : 16 * at + 16, features:] = pieces.astype(BF16)
        steered = rows * steer
        for b in range(features // HD):
            turned = two_piece_dot(steered[:, b * HD : (b + 1) * HD], matrix) * (1.0 / math.sqrt(HD))
            out_ref[16 * at : 16 * at + 16, b * HD : (b + 1) * HD] = turned.astype(BF16)


def project_kernel(x0, x1, x2, x3, weight, out_ref):
    parts, width = 3, weight.shape[1] // 3
    features = weight.shape[0]
    x, c = lax.axis_index("x"), lax.axis_index("core")
    received = (x0, x1, x2, x3)
    targets = []
    for s in range(4):
        for other in range(2):
            core = c if other == 0 else 1 - c
            source = 2 * (x ^ s) + core
            targets += [2 * source, 2 * source + 1]
    for s in range(4):
        extra = received[s][:, features:].astype(F32)
        for j in range(4):
            out_ref[targets[4 * s + j], :, weight.shape[1] :] = extra[8 * j : 8 * j + 8].astype(BF16)
    rows = jnp.concatenate([r[:, :features] for r in received], axis=0)
    for i in range(parts):
        product = jnp.dot(rows, weight[:, i * width : (i + 1) * width], preferred_element_type=F32)
        for j in range(16):
            out_ref[targets[j], :, i * width : (i + 1) * width] = product[8 * j : 8 * j + 8].astype(BF16)


COVER = (30, 1, 10)
TILE = 1024


def attend_kernel(
    lengths_ref, arrived_ref, cos_ref, sin_ref, sign_ref, keys, values, out_ref, queries, scores, attended
):
    lists, slots = keys.shape[0], keys.shape[2]
    total = arrived_ref[0].astype(F32)
    for w in range(1, arrived_ref.shape[0]):
        total = total + arrived_ref[w].astype(F32)
    columns = (QG + 2) * HD
    squares = jnp.sum(total[:, columns:], axis=1, keepdims=True)
    factor = lax.rsqrt(squares * (1.0 / D) + 1e-05)
    cosine, sine = cos_ref[...], sin_ref[...]
    for h in range(QG + 2):
        vector = total[:, h * HD : (h + 1) * HD] * factor
        if h <= QG:
            vector = vector * cosine + pltpu.roll(vector, HD // 2, 1) * sine
        queries[:, h, :] = vector.astype(BF16).astype(F32)

    scale = math.log2(math.e) / math.sqrt(HD)
    lane = lax.broadcasted_iota(jnp.int32, (QG, HD), 1)
    spans = [slice(start, start + TILE) for start in range(0, slots, TILE)]
    query, fresh, peak = [], [], []
    for i in range(lists):
        heads = queries[i]
        query.append(heads[:QG].astype(BF16))
        fresh.append(jnp.sum(heads[:QG] * heads[QG : QG + 1], axis=1, keepdims=True) * scale)
        peak.append(jnp.full((QG, HD), -1e30, F32))
    for span in spans:
        for i in range(lists):
            block = lax.dot_general(
                query[i], keys[i, 0, span, :], (((1,), (1,)), ((), ())), preferred_element_type=F32
            )
            length = jnp.broadcast_to(lengths_ref[i : i + 1, :], (QG, HD))
            for t in range(TILE // HD):
                at = span.start + t * HD
                piece = jnp.where(lane < length - at, block[:, t * HD : (t + 1) * HD] * scale, -1e30)
                scores[i, :, at : at + HD] = piece
                peak[i] = jnp.maximum(peak[i], piece)
    peak = [jnp.maximum(jnp.max(peak[i], axis=1, keepdims=True), fresh[i]) for i in range(lists)]
    mass = [jnp.zeros((QG, HD), F32)] * lists
    mixed = [jnp.zeros((QG, HD), F32)] * lists
    for span in spans:
        for i in range(lists):
            weight = jnp.exp2(scores[i, :, span] - peak[i])
            for t in range(TILE // HD):
                mass[i] = mass[i] + weight[:, t * HD : (t + 1) * HD]
            mixed[i] = mixed[i] + jnp.dot(weight.astype(BF16), values[i, 0, span, :], preferred_element_type=F32)
    for i in range(lists):
        weight_new = jnp.exp2(fresh[i] - peak[i])
        denominator = jnp.sum(mass[i], axis=1, keepdims=True) + weight_new
        added = weight_new.astype(BF16).astype(F32) * queries[i, QG + 1 : QG + 2, :]
        attended[QG * i : QG * (i + 1), :] = (mixed[i] + added) / denominator

    matrix = hadamard_signs()
    steered = []
    for h in range(QG):
        steered.append(attended[pl.ds(h, lists, stride=QG), :] * sign_ref[:, h * HD : (h + 1) * HD])
    turned = two_piece_dot(jnp.concatenate(steered, axis=0), matrix) * (1.0 / math.sqrt(HD))
    for h in range(QG):
        piece = turned[lists * h : lists * (h + 1)].astype(BF16)
        for w in range(out_ref.shape[0]):
            out_ref[w, :, h * HD : (h + 1) * HD] = piece


def mix_kernel(rows_ref, weight, keep_ref, send_ref):
    parts, width = 4, weight.shape[1] // 4
    c = lax.axis_index("core")
    rows = jnp.concatenate([rows_ref[x, c] for x in range(4)] + [rows_ref[x, 1 - c] for x in range(4)], axis=0)
    for i in range(parts):
        product = jnp.dot(rows, weight[:, i * width : (i + 1) * width], preferred_element_type=F32)
        for x in range(4):
            keep_ref[x, :, i * width : (i + 1) * width] = product[16 * x : 16 * x + 16]
            send_ref[x, :, i * width : (i + 1) * width] = product[64 + 16 * x : 80 + 16 * x].astype(BF16)


def pair_sum_kernel(keep_ref, got_ref, own_ref, s1, s2, s3):
    x = lax.axis_index("x")
    own_ref[...] = keep_ref[x] + got_ref[x].astype(F32)
    for s, ref in ((1, s1), (2, s2), (3, s3)):
        to = x ^ s
        ref[...] = (keep_ref[to] + got_ref[to].astype(F32)).astype(BF16)


def last_kernel(hidden_ref, own_ref, r1, r2, r3, out_ref):
    mixed = own_ref[...] + r1[...].astype(F32) + r2[...].astype(F32) + r3[...].astype(F32)
    out_ref[...] = (hidden_ref[...].astype(F32) + mixed).astype(BF16)


def params(limit):
    return pltpu.CompilerParams(vmem_limit_bytes=limit * MIB)


def cost(microseconds):
    return pl.CostEstimate(flops=int(microseconds * 1.1e9), transcendentals=0, bytes_accessed=int(microseconds * 3e6))


def along_x(values):
    return [lax.ppermute(v, "x", [(i, i ^ s) for i in range(4)]) for s, v in zip((1, 2, 3), values)]


def across_cores(value):
    return lax.ppermute(value, "core", [(0, 1), (1, 0)])


def body(hidden, gain, sign_in, qkv_weight, out_weight, sign_attn, key_cache, value_cache, lengths):
    rows, features = hidden.shape
    columns = qkv_weight.shape[1]
    own_lists, _, slots, _ = key_cache.shape
    peers = lax.axis_size(WIDE)

    steer = gain.astype(F32) * (2 * sign_in - 1).astype(F32)
    rotated = pl.pallas_call(
        rotate_in_kernel,
        out_shape=jax.ShapeDtypeStruct((2 * rows, features + EXTRA), BF16),
        in_specs=[VMEM] * 3,
        out_specs=VMEM,
        compiler_params=params(2),
        cost_estimate=cost(COVER[0]),
        name="rotate_in",
    )(hidden.astype(F32), across_cores(hidden), steer.reshape(1, -1))
    rotated, lengths, sign_attn = lax.optimization_barrier((rotated, lengths, sign_attn))
    frequency = jnp.exp(jnp.arange(HD // 2, dtype=F32) * (-2.0 * math.log(ROPE_BASE) / HD))
    angles = lengths.astype(F32)[:, None] * frequency[None, :]
    cosine, sine = jnp.cos(angles), jnp.sin(angles)
    cosine = jnp.concatenate([cosine, cosine], axis=1)
    sine = jnp.concatenate([-sine, sine], axis=1)
    sign_out = (2 * sign_attn - 1).astype(F32).reshape(1, -1)
    received = along_x([rotated] * 3)
    received, cosine, sine, sign_out, lengths = lax.optimization_barrier((received, cosine, sine, sign_out, jnp.broadcast_to(lengths[:, None], (own_lists, HD))))
    partial = pl.pallas_call(
        project_kernel,
        out_shape=jax.ShapeDtypeStruct((peers, own_lists, columns + EXTRA), BF16),
        in_specs=[VMEM] * 5,
        out_specs=VMEM,
        compiler_params=params(2),
        cost_estimate=cost(COVER[1]),
        name="project",
    )(rotated, *received, qkv_weight)
    arrived = lax.all_to_all(partial, WIDE, split_axis=0, concat_axis=0, tiled=True)

    sent = pl.pallas_call(
        attend_kernel,
        out_shape=jax.ShapeDtypeStruct((peers, own_lists, QG * HD), BF16),
        in_specs=[VMEM] * 7,
        out_specs=VMEM,
        scratch_shapes=[
            pltpu.VMEM((own_lists, 24, HD), F32),
            pltpu.VMEM((own_lists, QG, slots), F32),
            pltpu.VMEM((own_lists * QG, HD), F32),
        ],
        compiler_params=params(6),
        cost_estimate=cost(COVER[2]),
        name="attend",
    )(
        lengths,
        arrived,
        cosine,
        sine,
        sign_out,
        key_cache,
        value_cache,
    )
    gathered = lax.all_to_all(sent, WIDE, split_axis=0, concat_axis=0, tiled=True)
    keep, send = pl.pallas_call(
        mix_kernel,
        out_shape=(
            jax.ShapeDtypeStruct((4, rows, features), F32),
            jax.ShapeDtypeStruct((4, rows, features), BF16),
        ),
        in_specs=[VMEM, VMEM],
        out_specs=(VMEM, VMEM),
        compiler_params=params(2),
        name="mix",
    )(gathered.reshape(4, 2, rows, QG * HD), out_weight)
    own, *sends = pl.pallas_call(
        pair_sum_kernel,
        out_shape=(jax.ShapeDtypeStruct((rows, features), F32),)
        + (jax.ShapeDtypeStruct((rows, features), BF16),) * 3,
        in_specs=[VMEM, VMEM],
        out_specs=(VMEM,) * 4,
        compiler_params=params(2),
        name="pair_sum",
    )(keep, across_cores(send))
    got = along_x(sends)
    return pl.pallas_call(
        last_kernel,
        out_shape=jax.ShapeDtypeStruct((rows, features), BF16),
        in_specs=[VMEM] * 5,
        out_specs=VMEM,
        compiler_params=params(2),
        name="last",
    )(hidden, own, *got)


def solution(mesh):
    split = Mesh(mesh.devices.reshape(4, 4, 4, 2), ("y", "z", "x", "core"))
    narrow = ("x", "core")
    placed = (
        P(narrow, WIDE),
        P(WIDE),
        P(WIDE),
        P(WIDE, narrow),
        P(narrow, WIDE),
        P(narrow),
        P(WIDE, narrow, None, None),
        P(WIDE, narrow, None, None),
        P(WIDE),
    )
    return jax.shard_map(
        body, mesh=split, in_specs=placed, out_specs=P(narrow, WIDE), check_vma=False
    )
```

```python
import math

import jax
import jax.numpy as jnp
from jax import lax
from jax.experimental import pallas as pl
from jax.experimental.pallas import tpu as pltpu
from jax.sharding import Mesh
from jax.sharding import PartitionSpec as P

D = 16384
HD = 128
QG = 16
WIDE = ("y", "z")
ROPE_BASE = 500000.0
EXTRA = 128
MIB = 1 << 20
VMEM = pl.BlockSpec(memory_space=pltpu.VMEM)
HBM = pl.BlockSpec(memory_space=pl.ANY)
F32 = jnp.float32
BF16 = jnp.bfloat16


def hadamard_signs():
    common = lax.broadcasted_iota(jnp.int32, (HD, HD), 0) & lax.broadcasted_iota(jnp.int32, (HD, HD), 1)
    common = common ^ (common >> 4)
    common = common ^ (common >> 2)
    common = common ^ (common >> 1)
    return (1 - 2 * (common & 1)).astype(F32).astype(BF16)


def two_piece_dot(values, matrix):
    high = values.astype(BF16)
    low = (values - high.astype(F32)).astype(BF16)
    return jnp.dot(high, matrix, preferred_element_type=F32) + jnp.dot(low, matrix, preferred_element_type=F32)


def rotate_in_kernel(own_ref, other_ref, steer_ref, out_ref):
    features = own_ref.shape[1]
    matrix = hadamard_signs()
    steer = steer_ref[...]
    lane = lax.broadcasted_iota(jnp.int32, (16, EXTRA), 1)
    blocks = []
    for at, ref in enumerate((own_ref, other_ref)):
        rows = ref[...].astype(F32)
        squares = jnp.sum(rows * rows, axis=1, keepdims=True)
        first = squares.astype(BF16).astype(F32)
        second = (squares - first).astype(BF16).astype(F32)
        third = squares - first - second
        pieces = jnp.where(lane == 0, first, jnp.where(lane == 1, second, jnp.where(lane == 2, third, 0.0)))
        out_ref[16 * at : 16 * at + 16, features:] = pieces.astype(BF16)
        steered = rows * steer
        blocks += [steered[:, b * HD : (b + 1) * HD] for b in range(features // HD)]
    turned = two_piece_dot(jnp.concatenate(blocks, axis=0), matrix) * (1.0 / math.sqrt(HD))
    for i in range(len(blocks)):
        at, b = divmod(i, features // HD)
        out_ref[16 * at : 16 * at + 16, b * HD : (b + 1) * HD] = turned[16 * i : 16 * i + 16].astype(BF16)


def project_kernel(x0, x1, x2, x3, weight, out_ref):
    parts, width = 3, weight.shape[1] // 3
    features = weight.shape[0]
    x, c = lax.axis_index("x"), lax.axis_index("core")
    received = (x0, x1, x2, x3)
    targets = []
    for s in range(4):
        for other in range(2):
            core = c if other == 0 else 1 - c
            source = 2 * (x ^ s) + core
            targets += [2 * source, 2 * source + 1]
    for s in range(4):
        extra = received[s][:, features:].astype(F32)
        for j in range(4):
            out_ref[targets[4 * s + j], :, weight.shape[1] :] = extra[8 * j : 8 * j + 8].astype(BF16)
    rows = jnp.concatenate([r[:, :features] for r in received], axis=0)
    for i in range(parts):
        product = jnp.dot(rows, weight[:, i * width : (i + 1) * width], preferred_element_type=F32)
        for j in range(16):
            out_ref[targets[j], :, i * width : (i + 1) * width] = product[8 * j : 8 * j + 8].astype(BF16)


COVER = (30, 1, 10)
TILE = 1024


def attend_kernel(
    lengths_ref, arrived_ref, cos_ref, sin_ref, sign_ref, keys, values, out_ref, queries, scores, attended
):
    lists, slots = keys.shape[0], keys.shape[2]
    total = arrived_ref[0].astype(F32)
    for w in range(1, arrived_ref.shape[0]):
        total = total + arrived_ref[w].astype(F32)
    columns = (QG + 2) * HD
    squares = jnp.sum(total[:, columns:], axis=1, keepdims=True)
    factor = lax.rsqrt(squares * (1.0 / D) + 1e-05)
    cosine, sine = cos_ref[...] * factor, sin_ref[...] * factor
    for h in range(QG + 2):
        vector = total[:, h * HD : (h + 1) * HD]
        if h <= QG:
            vector = vector * cosine + pltpu.roll(vector, HD // 2, 1) * sine
        else:
            vector = vector * factor
        queries[:, h, :] = vector.astype(BF16).astype(F32)

    scale = math.log2(math.e) / math.sqrt(HD)
    lane = lax.broadcasted_iota(jnp.int32, (QG, HD), 1)
    spans = [slice(start, start + TILE) for start in range(0, slots, TILE)]
    query, fresh, peak = [], [], []
    for i in range(lists):
        heads = queries[i]
        query.append(heads[:QG].astype(BF16))
        fresh.append(jnp.sum(heads[:QG] * heads[QG : QG + 1], axis=1, keepdims=True) * scale)
        peak.append(jnp.full((QG, HD), -1e30, F32))
    for span in spans:
        for i in range(lists):
            block = lax.dot_general(
                query[i], keys[i, 0, span, :], (((1,), (1,)), ((), ())), preferred_element_type=F32
            )
            length = jnp.broadcast_to(lengths_ref[i : i + 1, :], (QG, HD))
            for t in range(TILE // HD):
                at = span.start + t * HD
                piece = jnp.where(lane < length - at, block[:, t * HD : (t + 1) * HD] * scale, -1e30)
                scores[i, :, at : at + HD] = piece
                peak[i] = jnp.maximum(peak[i], piece)
    peak = [jnp.maximum(jnp.max(peak[i], axis=1, keepdims=True), fresh[i]) for i in range(lists)]
    mass = [jnp.zeros((QG, HD), F32)] * lists
    mixed = [jnp.zeros((QG, HD), F32)] * lists
    for span in spans:
        for i in range(lists):
            weight = jnp.exp2(scores[i, :, span] - peak[i])
            for t in range(TILE // HD):
                mass[i] = mass[i] + weight[:, t * HD : (t + 1) * HD]
            mixed[i] = mixed[i] + jnp.dot(weight.astype(BF16), values[i, 0, span, :], preferred_element_type=F32)
    for i in range(lists):
        weight_new = jnp.exp2(fresh[i] - peak[i])
        denominator = jnp.sum(mass[i], axis=1, keepdims=True) + weight_new
        added = weight_new.astype(BF16).astype(F32) * queries[i, QG + 1 : QG + 2, :]
        attended[QG * i : QG * (i + 1), :] = (mixed[i] + added) / denominator

    matrix = hadamard_signs()
    steered = []
    for h in range(QG):
        steered.append(attended[pl.ds(h, lists, stride=QG), :] * sign_ref[:, h * HD : (h + 1) * HD])
    turned = two_piece_dot(jnp.concatenate(steered, axis=0), matrix) * (1.0 / math.sqrt(HD))
    for h in range(QG):
        piece = turned[lists * h : lists * (h + 1)].astype(BF16)
        for w in range(out_ref.shape[0]):
            out_ref[w, :, h * HD : (h + 1) * HD] = piece


def mix_kernel(rows_ref, weight, keep_ref, send_ref):
    parts, width = 4, weight.shape[1] // 4
    c = lax.axis_index("core")
    rows = jnp.concatenate([rows_ref[x, c] for x in range(4)] + [rows_ref[x, 1 - c] for x in range(4)], axis=0)
    for i in range(parts):
        product = jnp.dot(rows, weight[:, i * width : (i + 1) * width], preferred_element_type=F32)
        for x in range(4):
            keep_ref[x, :, i * width : (i + 1) * width] = product[16 * x : 16 * x + 16]
            send_ref[x, :, i * width : (i + 1) * width] = product[64 + 16 * x : 80 + 16 * x].astype(BF16)


def pair_sum_kernel(keep_ref, got_ref, own_ref, s1, s2, s3):
    x = lax.axis_index("x")
    own_ref[...] = keep_ref[x] + got_ref[x].astype(F32)
    for s, ref in ((1, s1), (2, s2), (3, s3)):
        to = x ^ s
        ref[...] = (keep_ref[to] + got_ref[to].astype(F32)).astype(BF16)


def last_kernel(hidden_ref, own_ref, r1, r2, r3, out_ref):
    mixed = own_ref[...] + r1[...].astype(F32) + r2[...].astype(F32) + r3[...].astype(F32)
    out_ref[...] = (hidden_ref[...].astype(F32) + mixed).astype(BF16)


def params(limit):
    return pltpu.CompilerParams(vmem_limit_bytes=limit * MIB)


def cost(microseconds):
    return pl.CostEstimate(flops=int(microseconds * 1.1e9), transcendentals=0, bytes_accessed=int(microseconds * 3e6))


def along_x(values):
    return [lax.ppermute(v, "x", [(i, i ^ s) for i in range(4)]) for s, v in zip((1, 2, 3), values)]


def across_cores(value):
    return lax.ppermute(value, "core", [(0, 1), (1, 0)])


def body(hidden, gain, sign_in, qkv_weight, out_weight, sign_attn, key_cache, value_cache, lengths):
    rows, features = hidden.shape
    columns = qkv_weight.shape[1]
    own_lists, _, slots, _ = key_cache.shape
    peers = lax.axis_size(WIDE)

    steer = gain.astype(F32) * (2 * sign_in - 1).astype(F32)
    rotated = pl.pallas_call(
        rotate_in_kernel,
        out_shape=jax.ShapeDtypeStruct((2 * rows, features + EXTRA), BF16),
        in_specs=[VMEM] * 3,
        out_specs=VMEM,
        compiler_params=params(2),
        cost_estimate=cost(COVER[0]),
        name="rotate_in",
    )(hidden.astype(F32), across_cores(hidden), steer.reshape(1, -1))
    rotated, lengths, sign_attn = lax.optimization_barrier((rotated, lengths, sign_attn))
    frequency = jnp.exp(jnp.arange(HD // 2, dtype=F32) * (-2.0 * math.log(ROPE_BASE) / HD))
    angles = lengths.astype(F32)[:, None] * frequency[None, :]
    cosine, sine = jnp.cos(angles), jnp.sin(angles)
    cosine = jnp.concatenate([cosine, cosine], axis=1)
    sine = jnp.concatenate([-sine, sine], axis=1)
    sign_out = (2 * sign_attn - 1).astype(F32).reshape(1, -1)
    received = along_x([rotated] * 3)
    received, cosine, sine, sign_out, lengths = lax.optimization_barrier((received, cosine, sine, sign_out, jnp.broadcast_to(lengths[:, None], (own_lists, HD))))
    partial = pl.pallas_call(
        project_kernel,
        out_shape=jax.ShapeDtypeStruct((peers, own_lists, columns + EXTRA), BF16),
        in_specs=[VMEM] * 5,
        out_specs=VMEM,
        compiler_params=params(2),
        cost_estimate=cost(COVER[1]),
        name="project",
    )(rotated, *received, qkv_weight)
    arrived = lax.all_to_all(partial, WIDE, split_axis=0, concat_axis=0, tiled=True)

    sent = pl.pallas_call(
        attend_kernel,
        out_shape=jax.ShapeDtypeStruct((peers, own_lists, QG * HD), BF16),
        in_specs=[VMEM] * 7,
        out_specs=VMEM,
        scratch_shapes=[
            pltpu.VMEM((own_lists, 24, HD), F32),
            pltpu.VMEM((own_lists, QG, slots), F32),
            pltpu.VMEM((own_lists * QG, HD), F32),
        ],
        compiler_params=params(6),
        cost_estimate=cost(COVER[2]),
        name="attend",
    )(
        lengths,
        arrived,
        cosine,
        sine,
        sign_out,
        key_cache,
        value_cache,
    )
    gathered = lax.all_to_all(sent, WIDE, split_axis=0, concat_axis=0, tiled=True)
    keep, send = pl.pallas_call(
        mix_kernel,
        out_shape=(
            jax.ShapeDtypeStruct((4, rows, features), F32),
            jax.ShapeDtypeStruct((4, rows, features), BF16),
        ),
        in_specs=[VMEM, VMEM],
        out_specs=(VMEM, VMEM),
        compiler_params=params(2),
        name="mix",
    )(gathered.reshape(4, 2, rows, QG * HD), out_weight)
    own, *sends = pl.pallas_call(
        pair_sum_kernel,
        out_shape=(jax.ShapeDtypeStruct((rows, features), F32),)
        + (jax.ShapeDtypeStruct((rows, features), BF16),) * 3,
        in_specs=[VMEM, VMEM],
        out_specs=(VMEM,) * 4,
        compiler_params=params(2),
        name="pair_sum",
    )(keep, across_cores(send))
    got = along_x(sends)
    return pl.pallas_call(
        last_kernel,
        out_shape=jax.ShapeDtypeStruct((rows, features), BF16),
        in_specs=[VMEM] * 5,
        out_specs=VMEM,
        compiler_params=params(2),
        name="last",
    )(hidden, own, *got)


def solution(mesh):
    split = Mesh(mesh.devices.reshape(4, 4, 4, 2), ("y", "z", "x", "core"))
    narrow = ("x", "core")
    placed = (
        P(narrow, WIDE),
        P(WIDE),
        P(WIDE),
        P(WIDE, narrow),
        P(narrow, WIDE),
        P(narrow),
        P(WIDE, narrow, None, None),
        P(WIDE, narrow, None, None),
        P(WIDE),
    )
    return jax.shard_map(
        body, mesh=split, in_specs=placed, out_specs=P(narrow, WIDE), check_vma=False
    )
```
